256 devices in a mesh: row: 8 (over z), col: 16 (over y, x), smp: 2 (over core).
Axes of the slice: x: 4, y: 4, z: 8, core: 2. Of those that a mesh axis runs over, the one named last changes fastest.
Arguments:
- state: float32 [8, 2048, 512], P('smp', ('row', 'col')), may hold values from -6 to 6
- noise: float32 [2, 8, 2048, 512], P(None, 'smp', ('row', 'col')), may hold values from -6 to 6
- pair: bfloat16 [2048, 2048, 128], P('row', 'col'), may hold values from -10 to 10
- contacts: int32 [16, 6], replicated, may hold values from -1 to 15, as said below
- norm_gain: float32 [512], replicated, may hold values from 0.1 to 1.9
- w_qkv: bfloat16 [512, 1536], replicated, may hold values from -0.25 to 0.25
- w_out: bfloat16 [512, 512], replicated, may hold values from -0.25 to 0.25
- w_bias: bfloat16 [128, 32], replicated, may hold values from -1.5 to 1.5
Outputs:
- denoised: float32 [8, 2048, 512], P('smp', ('row', 'col'))
The draws below stay inside these ranges and needn't reach their ends.
Inputs may be any that keep to these rules, and one draw needn't show every extreme that they name: `contacts`: row q lists distinct blocks, q itself first, then nearby blocks more often than far ones; its first counts are blocks and the remaining slots hold -1; some row uses all 6 slots.
All inputs are finite; a program needn't handle non-finite values.
Results may differ from the reference program's by a relative error of at most 0.012.
Values may be sent and summed in bfloat16 or wider, within the bound.
A program may use at most 128 MiB of HBM per device.

```python
from functools import partial
import jax
import jax.numpy as jnp
from jax import lax

DS = 512
CP = 128
HEADS = 32
SAMPLES = 8
STEPS = 2
HD = 16
L = 2048
BLK = 128
NBLK = 16
KMAX = 6


def contact_lists(key):
    key_order = jax.random.fold_in(key, 11)
    key_count = jax.random.fold_in(key, 12)
    key_full = jax.random.fold_in(key, 13)
    index = jnp.arange(NBLK, dtype=jnp.int32)
    distance = jnp.abs(index[:, None] - index[None, :])
    jitter = jax.random.randint(key_order, (NBLK, NBLK), 0, 4 * NBLK, dtype=jnp.int32)
    score = (jitter + 3 * distance) * NBLK + index[None, :]
    score = jnp.where(distance == 0, -1, score)
    order = jnp.argsort(score, axis=1, stable=True)[:, :KMAX].astype(jnp.int32)
    counts = jax.random.randint(key_count, (NBLK,), 1, KMAX + 1, dtype=jnp.int32)
    full_row = jax.random.randint(key_full, (), 0, NBLK, dtype=jnp.int32)
    counts = jnp.where(index == full_row, KMAX, counts)
    slots = jnp.arange(KMAX, dtype=jnp.int32)
    return jnp.where(slots[None, :] < counts[:, None], order, -1).astype(jnp.int32)


def draw_contacts(key, part):
    return contact_lists(key)


def bias_matrix(key):
    raw = jax.random.normal(jax.random.fold_in(key, 21), (CP, HEADS), jnp.float32)
    return jnp.clip(raw, -6.0, 6.0) * 0.25


def draw_w_bias(key, part):
    return bias_matrix(key).astype(jnp.bfloat16)


def draw_pair(key, part):
    raw = jax.random.normal(jax.random.fold_in(key, 31), (L, L, CP), jnp.float32)
    field = jnp.clip(raw, -6.0, 6.0)
    return field.astype(jnp.bfloat16)


def levels(key, extent, cuts, least, largest):
    level = 1.0
    for dim, shards_of in cuts:
        steps = jax.random.uniform(jax.random.fold_in(jax.random.fold_in(key, 6), dim), (shards_of,), jnp.float32, least / len(cuts), largest / len(cuts))
        level = level * jnp.repeat(jnp.exp(steps), extent[dim] // shards_of).reshape((-1,) + (1,) * (len(extent) - 1 - dim))
    return level


def bell_draw(key, shape, spread, bound, shards=(), held_as=jnp.bfloat16):
    drawn = spread * jax.random.normal(key, shape, jnp.float32)
    if shards:
        drawn = drawn * levels(key, shape, shards, -0.22, 0.18)
    return jnp.clip(drawn, -bound, bound).astype(held_as)


def setup_inputs(seed: int = 0) -> dict:
    key_list = jax.random.split(jax.random.key(seed), 9)
    return {
        "state": bell_draw(key_list[0], (SAMPLES, L, DS), 1.0, 6.0, ((0, 2), (1, 128)), jnp.float32),
        "noise": bell_draw(key_list[1], (STEPS, SAMPLES, L, DS), 1.0, 6.0, ((1, 2), (2, 128)), jnp.float32),
        "pair": draw_pair(jax.random.fold_in(key_list[8], 71), 0),
        "contacts": draw_contacts(jax.random.fold_in(key_list[8], 71), 0),
        "norm_gain": jnp.clip(1.0 + 0.18 * jax.random.normal(key_list[4], (DS,), jnp.float32), 0.1, 1.9),
        "w_qkv": bell_draw(key_list[5], (DS, 3 * DS), DS ** -0.5, 0.25),
        "w_out": bell_draw(key_list[6], (DS, DS), DS ** -0.5, 0.25),
        "w_bias": draw_w_bias(jax.random.fold_in(key_list[8], 71), 0),
    }


def query_block(qblock, queries, keys, values, pair, contacts, w_bias):
    start = qblock * BLK
    pair_rows = lax.dynamic_slice_in_dim(pair, start, BLK, 0).astype(jnp.float32)
    bias = jnp.einsum('ijc,ch->hij', pair_rows, w_bias.astype(jnp.float32)).astype(jnp.bfloat16)
    bias = lax.optimization_barrier(bias).astype(jnp.float32)
    q_rows = lax.dynamic_slice_in_dim(queries, start, BLK, 1).astype(jnp.float32)
    scores = jnp.einsum('srhd,skhd->hsrk', q_rows, keys.astype(jnp.float32)) * 0.25 + bias[:, None]
    scores = scores.reshape(HEADS, SAMPLES, BLK, NBLK, BLK)
    listed = contacts[qblock]
    allowed = jnp.any(listed[:, None] == jnp.arange(NBLK, dtype=jnp.int32)[None, :], axis=0)
    m_raw = lax.optimization_barrier(jnp.max(scores, axis=-1))
    m_blk = jnp.where(allowed, m_raw, jnp.float32(-1e+30))
    probs = jnp.where(allowed[:, None], jnp.exp(scores - m_raw[..., None]), jnp.float32(0.0))
    totals = lax.optimization_barrier(jnp.sum(probs, axis=-1))
    rounded = lax.optimization_barrier(probs.astype(jnp.bfloat16)).astype(jnp.float32)
    v_blocks = values.reshape(SAMPLES, NBLK, BLK, HEADS, HD).astype(jnp.float32)
    outputs = jnp.einsum('hsrnk,snkhd->hsrnd', rounded, v_blocks)
    top = lax.optimization_barrier(jnp.max(m_blk, axis=-1))
    weight = jnp.exp(m_blk - top[..., None])
    outputs = lax.optimization_barrier(jnp.sum(outputs * weight[..., None], axis=3))
    totals = lax.optimization_barrier(jnp.sum(totals * weight, axis=-1))
    attn = outputs / totals[..., None]
    return attn.transpose(1, 2, 0, 3).reshape(SAMPLES, BLK, DS).astype(jnp.bfloat16)

def reference(state, noise, pair, contacts, norm_gain, w_qkv, w_out, w_bias):
    x = state
    for step in range(STEPS):
        mean = lax.optimization_barrier(jnp.mean(x, axis=-1, keepdims=True))
        var = lax.optimization_barrier(jnp.mean((x - mean) ** 2, axis=-1, keepdims=True))
        normed = ((x - mean) * lax.rsqrt(var + 1e-05) * norm_gain).astype(jnp.bfloat16)
        qkv = jnp.dot(normed.reshape(SAMPLES * L, DS), w_qkv, preferred_element_type=jnp.float32)
        qkv = qkv.astype(jnp.bfloat16).reshape(SAMPLES, L, 3 * DS)
        queries = qkv[..., :DS].reshape(SAMPLES, L, HEADS, HD)
        keys = qkv[..., DS:2 * DS].reshape(SAMPLES, L, HEADS, HD)
        values = qkv[..., 2 * DS:].reshape(SAMPLES, L, HEADS, HD)
        worker = partial(query_block, queries=queries, keys=keys, values=values, pair=pair, contacts=contacts, w_bias=w_bias)
        blocks = lax.map(worker, jnp.arange(NBLK, dtype=jnp.int32))
        attn = blocks.transpose(1, 0, 2, 3).reshape(SAMPLES * L, DS)
        out = jnp.dot(attn, w_out, preferred_element_type=jnp.float32).reshape(SAMPLES, L, DS)
        x = x + out + 0.5 * 0.5 ** step * noise[step]
    return x
```

```python
import jax
import jax.numpy as jnp
from jax import lax
from jax.experimental import pallas as pl
from jax.experimental.pallas import tpu as pltpu
from jax.sharding import PartitionSpec as P


STEPS = 2
NZ, NC = 8, 16
SAMP, ROWS, DS = 4, 16, 512
HEADS, HD, CP = 32, 16, 128
BLK, KMAX = 128, 6
KEYS = KMAX * BLK
CHUNKS = 8
CH = BLK // CHUNKS
MESH = pl.DeviceIdType.MESH
BF, F32 = jnp.bfloat16, jnp.float32
NT = (((1,), (1,)), ((), ()))

OFFSETS = sorted(
    ((dy, dx) for dy in range(4) for dx in range(4) if (dy, dx) != (0, 0)),
    key=lambda o: -(min(o[0], 4 - o[0]) + min(o[1], 4 - o[1])),
)


def swap4(tiles, lane):
    a, b, c, d = tiles
    low = lane < 64
    a, c = jnp.where(low, a, pltpu.roll(c, 64, 1)), jnp.where(low, pltpu.roll(a, 64, 1), c)
    b, d = jnp.where(low, b, pltpu.roll(d, 64, 1)), jnp.where(low, pltpu.roll(b, 64, 1), d)
    even = (lane // 32) % 2 == 0
    a, b = jnp.where(even, a, pltpu.roll(b, 32, 1)), jnp.where(even, pltpu.roll(a, 96, 1), b)
    c, d = jnp.where(even, c, pltpu.roll(d, 32, 1)), jnp.where(even, pltpu.roll(c, 96, 1), d)
    return a, b, c, d


def kernel(
    state_ref, noise_ref, pair_ref, contacts_ref, gain_ref, wqkv_ref, wout_ref, wb_ref, out_ref,
    x_ref, pair_buf, stage, bias_send, bias_all, biasf, qkv_send, q_all, kv_first, kv_second, kcat, vcat,
    num, den, attn_send, attn_recv,
    pair_sem, bsend_sem, brecv_sem, fsend_sem, frecv_sem,
    kvsend_sem, kvrecv_sem, qsend_sem, qrecv_sem, local_sem,
    ring_send, ring_recv, asend_sem, arecv_sem,
):
    z, c, s = lax.axis_index("row"), lax.axis_index("col"), lax.axis_index("smp")
    y, x0 = c // 4, c % 4
    kv_all = (kv_first, kv_second)

    def col_at(o, sign):
        return ((y + sign * o[0] + 4) % 4) * 4 + (x0 + sign * o[1] + 4) % 4

    def drain(ref, sem):
        pltpu.make_async_copy(ref, ref, sem).wait()

    barrier = pltpu.get_barrier_semaphore()
    for o in OFFSETS:
        pl.semaphore_signal(barrier, inc=1, device_id={"col": col_at(o, 1)}, device_id_type=MESH)
    right, left = (z + 1) % NZ, (z + NZ - 1) % NZ
    pl.semaphore_signal(barrier, inc=1, device_id={"row": right}, device_id_type=MESH)
    pl.semaphore_signal(barrier, inc=1, device_id={"row": left}, device_id_type=MESH)
    pl.semaphore_signal(barrier, inc=1, device_id={"smp": 1 - s}, device_id_type=MESH)

    def pair_copy(ch):
        return pltpu.make_async_copy(
            pair_ref.at[pl.ds(s * BLK + ch * CH, CH)], pair_buf.at[pl.ds(ch * CH, CH)], pair_sem.at[ch]
        )

    for ch in range(CHUNKS):
        pair_copy(ch).start()

    lane = lax.broadcasted_iota(jnp.int32, (ROWS, 128), 1)

    def project(step):
        x = x_ref[...]
        mean = jnp.mean(x, axis=-1, keepdims=True)
        var = jnp.mean((x - mean) ** 2, axis=-1, keepdims=True)
        h = ((x - mean) * lax.rsqrt(var + 1e-05) * gain_ref[...]).astype(BF)
        for part in (1, 2, 0):
            y3 = jnp.dot(h, wqkv_ref[:, part * DS : (part + 1) * DS], preferred_element_type=F32)
            if part == 0:
                y3 = y3 * 0.25
            for t in range(4):
                tiles = [y3[k * ROWS : (k + 1) * ROWS, t * 128 : (t + 1) * 128] for k in range(SAMP)]
                for u, tile in enumerate(swap4(tiles, lane)):
                    qkv_send[step, 4 * t + u, part] = tile.astype(BF)

    def kv_slot(step, col):
        return kv_all[step].at[2 * z + col // 8, :, pl.ds(pl.multiple_of((col % 8) * ROWS, ROWS), ROWS), :]

    def rows_of(col):
        return pl.ds(pl.multiple_of(col * ROWS, ROWS), ROWS)

    def spread(step):
        half = c // 8
        for o in OFFSETS:
            to = col_at(o, 1)
            pltpu.make_async_remote_copy(
                src_ref=qkv_send.at[step, to, pl.ds(1, 2)],
                dst_ref=kv_slot(step, c),
                send_sem=kvsend_sem.at[step],
                recv_sem=kvrecv_sem.at[step, half],
                device_id={"col": to},
                device_id_type=MESH,
            ).start()
        pltpu.make_async_copy(
            qkv_send.at[step, c, pl.ds(1, 2)], kv_slot(step, c), kvrecv_sem.at[step, half]
        ).start()
        for o in OFFSETS:
            to = col_at(o, 1)
            pltpu.make_async_remote_copy(
                src_ref=qkv_send.at[step, to, 0],
                dst_ref=q_all.at[step, rows_of(c), :],
                send_sem=qsend_sem.at[step],
                recv_sem=qrecv_sem.at[step],
                device_id={"col": to},
                device_id_type=MESH,
            ).start()
        pltpu.make_async_copy(
            qkv_send.at[step, c, 0], q_all.at[step, rows_of(c), :], qrecv_sem.at[step]
        ).start()

    def ring_copy(step, way, t, j, plane):
        ref = kv_all[step].at[2 * plane + j // 2, j % 2]
        return pltpu.make_async_remote_copy(
            src_ref=ref,
            dst_ref=ref,
            send_sem=ring_send.at[step, way, t, j],
            recv_sem=ring_recv.at[step, way, t, j],
            device_id={"row": right if way == 0 else left},
            device_id_type=MESH,
        )

    def ring_plane(way, t):
        return (z - t + NZ) % NZ if way == 0 else (z + t) % NZ

    def ring_used(way, t, j):
        return t < 3 or (j < 2) == (way == 0)

    def ring(step):
        for t in range(4):
            for j in range(4):
                if t == 0 and j % 2 == 0:
                    drain(kv_all[step].at[2 * z + j // 2], kvrecv_sem.at[step, j // 2])
                for way in range(2):
                    if not ring_used(way, t, j):
                        continue
                    if t > 0:
                        ring_copy(step, way, t - 1, j, ring_plane(way, t)).wait_recv()
                    ring_copy(step, way, t, j, ring_plane(way, t)).start()

    def ring_finish(step):
        for way in range(2):
            for t in (2, 3):
                for j in range(4):
                    if ring_used(way, t, j) and not (t == 2 and ring_used(way, 3, j)):
                        ring_copy(step, way, t, j, ring_plane(way, t + 1)).wait_recv()

    def make_bias():
        wt = wb_ref[...].astype(F32).T.astype(BF)

        def chunk(ch, carry):
            pair_copy(ch).wait()
            for i in range(CH):
                stage[i * HEADS : (i + 1) * HEADS, :] = lax.dot_general(
                    wt, pair_buf[ch * CH + i], NT, preferred_element_type=F32
                )
            for h in range(HEADS):
                tile = stage[pl.ds(h, CH, stride=HEADS), :]
                bias_send[h // 2, h % 2, pl.ds(pl.multiple_of(ch * CH, CH), CH), :] = tile.astype(BF)
            return carry

        lax.fori_loop(0, CHUNKS, chunk, 0)

    def send_bias():
        for o in OFFSETS:
            to = col_at(o, 1)
            pltpu.make_async_remote_copy(
                src_ref=bias_send.at[to],
                dst_ref=bias_all.at[s, c],
                send_sem=bsend_sem,
                recv_sem=brecv_sem.at[c],
                device_id={"col": to},
                device_id_type=MESH,
            ).start()
        pltpu.make_async_copy(bias_send.at[c], bias_all.at[s, c], brecv_sem.at[c]).start()

    def pass_bias(col):
        drain(bias_all.at[s, col], brecv_sem.at[col])
        pltpu.make_async_remote_copy(
            src_ref=bias_all.at[s, col],
            dst_ref=bias_all.at[s, col],
            send_sem=fsend_sem,
            recv_sem=frecv_sem,
            device_id={"smp": 1 - s},
            device_id_type=MESH,
        ).start()

    def widen_bias():
        for qb in range(2):
            for slot in range(KMAX):
                kb = contacts_ref[2 * z + qb, slot]
                at = jnp.maximum(kb, 0)
                for hh in range(2):
                    tile = bias_all[qb, at, hh].astype(F32)
                    tile = jnp.where(kb >= 0, tile, F32(-1e30))
                    biasf[qb, hh * BLK : (hh + 1) * BLK, slot * BLK : (slot + 1) * BLK] = tile

    def attend(step):
        for qb in range(2):
            for slot in range(KMAX):
                at = jnp.maximum(contacts_ref[2 * z + qb, slot], 0)
                kcat[qb, slot * BLK : (slot + 1) * BLK, :] = kv_all[step][at, 0]
                vcat[qb, slot * BLK : (slot + 1) * BLK, 0:128] = kv_all[step][at, 1]
        wide = lax.broadcasted_iota(jnp.int32, (BLK, 128), 1) // HD

        def unit(it, carry):
            qb, sample = it // 4, it % 4
            q = q_all[step, pl.ds(pl.multiple_of(qb * BLK, BLK), BLK), :]
            picks = [wide == 2 * sample + hh for hh in range(2)]
            qs = jnp.concatenate([q * pick.astype(F32).astype(BF) for pick in picks], axis=0)
            scores = lax.dot_general(qs, kcat[qb], NT, preferred_element_type=F32) + biasf[qb]
            top = jnp.max(scores, axis=-1, keepdims=True)
            probs = jnp.exp(scores - top).astype(BF)
            both = jnp.dot(probs, vcat[qb], preferred_element_type=F32)
            at = pl.ds(pl.multiple_of(qb * BLK, BLK), BLK)
            n, d = num[at, :], den[at, :]
            for hh in range(2):
                part = both[hh * BLK : (hh + 1) * BLK]
                n = jnp.where(picks[hh], part[:, :128], n)
                d = jnp.where(picks[hh], part[:, 128:], d)
            num[at, :] = n
            den[at, :] = d
            return carry

        lax.fori_loop(0, 8, unit, 0)
        attn_send[step] = (num[...] / den[...]).astype(BF)

    def give_back(step):
        for o in OFFSETS:
            to = col_at(o, 1)
            pltpu.make_async_remote_copy(
                src_ref=attn_send.at[step, rows_of(to), :],
                dst_ref=attn_recv.at[step, c],
                send_sem=asend_sem.at[step],
                recv_sem=arecv_sem.at[step],
                device_id={"col": to},
                device_id_type=MESH,
            ).start()
        pltpu.make_async_copy(
            attn_send.at[step, rows_of(c), :], attn_recv.at[step, c], arecv_sem.at[step]
        ).start()
        drain(attn_recv.at[step], arecv_sem.at[step])

    def update(step):
        columns = []
        for t in range(4):
            tiles = [attn_recv[step, 4 * t + u].astype(F32) for u in range(4)]
            columns.append(swap4(tiles, lane))
        attn = jnp.concatenate(
            [jnp.concatenate([columns[t][k] for t in range(4)], axis=1) for k in range(SAMP)], axis=0
        ).astype(BF)
        out = jnp.dot(attn, wout_ref[...], preferred_element_type=F32)
        return x_ref[...] + out + 0.5 * 0.5**step * noise_ref[step]

    x_ref[...] = state_ref[...]
    vcat[:, :, 128:] = jnp.ones((2, KEYS, 128), BF)
    num[...] = jnp.zeros_like(num)
    den[...] = jnp.ones_like(den)
    project(0)
    pl.semaphore_wait(barrier, len(OFFSETS) + 3)
    for step in range(STEPS):
        if step:
            project(step)
        spread(step)
        if step == 0:
            make_bias()
            send_bias()
        ring(step)
        if step == 0:
            pass_bias(c)
            for o in reversed(OFFSETS):
                pass_bias(col_at(o, -1))
            drain(bias_all.at[1 - s], frecv_sem)
            widen_bias()
        ring_finish(step)
        drain(q_all.at[step], qrecv_sem.at[step])
        attend(step)
        give_back(step)
        x = update(step)
        if step < STEPS - 1:
            x_ref[...] = x
        else:
            out_ref[...] = x

    drain(bias_send.at[pl.ds(0, NC - 1)], bsend_sem)
    drain(bias_all.at[0], fsend_sem)
    for step in range(STEPS):
        drain(qkv_send.at[step, pl.ds(0, NC - 1), pl.ds(1, 2)], kvsend_sem.at[step])
        drain(q_all.at[step, pl.ds(0, (NC - 1) * ROWS), :], qsend_sem.at[step])
        drain(attn_send.at[step, pl.ds(0, (NC - 1) * ROWS), :], asend_sem.at[step])
        for way in range(2):
            for t in range(4):
                for j in range(4):
                    if ring_used(way, t, j):
                        ring_copy(step, way, t, j, ring_plane(way, t)).wait_send()


def body(state, noise, pair, contacts, norm_gain, w_qkv, w_out, w_bias):
    vmem = pl.BlockSpec(memory_space=pltpu.VMEM)
    dma = pltpu.SemaphoreType.DMA
    out = pl.pallas_call(
        kernel,
        out_shape=jax.ShapeDtypeStruct((SAMP * ROWS, DS), F32),
        in_specs=[
            vmem, vmem, pl.BlockSpec(memory_space=pltpu.HBM), pl.BlockSpec(memory_space=pltpu.SMEM),
            vmem, vmem, vmem, vmem,
        ],
        out_specs=vmem,
        scratch_shapes=[
            pltpu.VMEM((SAMP * ROWS, DS), F32),
            pltpu.VMEM((BLK, BLK, CP), BF),
            pltpu.VMEM((CH * HEADS, BLK), F32),
            pltpu.VMEM((NC, 2, BLK, BLK), BF),
            pltpu.VMEM((2, NC, 2, BLK, BLK), BF),
            pltpu.VMEM((2, 2 * BLK, KEYS), F32),
            pltpu.VMEM((STEPS, NC, 3, ROWS, 128), BF),
            pltpu.VMEM((STEPS, 2 * BLK, 128), BF),
            pltpu.VMEM((NC, 2, BLK, 128), BF),
            pltpu.VMEM((NC, 2, BLK, 128), BF),
            pltpu.VMEM((2, KEYS, 128), BF),
            pltpu.VMEM((2, KEYS, 256), BF),
            pltpu.VMEM((2 * BLK, 128), F32),
            pltpu.VMEM((2 * BLK, 128), F32),
            pltpu.VMEM((STEPS, 2 * BLK, 128), BF),
            pltpu.VMEM((STEPS, NC, ROWS, 128), BF),
            dma((CHUNKS,)),
            dma,
            dma((NC,)),
            dma,
            dma,
            dma((STEPS,)),
            dma((STEPS, 2)),
            dma((STEPS,)),
            dma((STEPS,)),
            dma,
            dma((STEPS, 2, 4, 4)),
            dma((STEPS, 2, 4, 4)),
            dma((STEPS,)),
            dma((STEPS,)),
        ],
        compiler_params=pltpu.CompilerParams(
            collective_id=0, has_side_effects=True, vmem_limit_bytes=56 * 1024 * 1024
        ),
        name="denoise",
    )(
        state.reshape(SAMP * ROWS, DS),
        noise.reshape(STEPS, SAMP * ROWS, DS),
        pair,
        contacts,
        norm_gain.reshape(1, DS),
        w_qkv,
        w_out,
        w_bias,
    )
    return out.reshape(SAMP, ROWS, DS)


def solution(mesh):
    in_specs = (
        P("smp", ("row", "col"), None),
        P(None, "smp", ("row", "col"), None),
        P("row", "col", None),
        P(),
        P(),
        P(),
        P(),
        P(),
    )
    out_specs = P("smp", ("row", "col"), None)
    return jax.shard_map(body, mesh=mesh, in_specs=in_specs, out_specs=out_specs, check_vma=False)
```

```python
import jax
import jax.numpy as jnp
from jax import lax
from jax.experimental import pallas as pl
from jax.experimental.pallas import tpu as pltpu
from jax.sharding import PartitionSpec as P


STEPS = 2
NZ, NC = 8, 16
SAMP, ROWS, DS = 4, 16, 512
HEADS, HD, CP = 32, 16, 128
BLK, KMAX = 128, 6
KEYS = KMAX * BLK
CHUNKS = 8
CH = BLK // CHUNKS
PIECES = 1
J = 1
STRIP = 64
MESH = pl.DeviceIdType.MESH
BF, F32 = jnp.bfloat16, jnp.float32
NT = (((1,), (1,)), ((), ()))

OFFSETS = sorted(
    ((dy, dx) for dy in range(4) for dx in range(4) if (dy, dx) != (0, 0)),
    key=lambda o: -(min(o[0], 4 - o[0]) + min(o[1], 4 - o[1])),
)


def swap4(tiles, lane):
    a, b, c, d = tiles
    low = lane < 64
    a, c = jnp.where(low, a, pltpu.roll(c, 64, 1)), jnp.where(low, pltpu.roll(a, 64, 1), c)
    b, d = jnp.where(low, b, pltpu.roll(d, 64, 1)), jnp.where(low, pltpu.roll(b, 64, 1), d)
    even = (lane // 32) % 2 == 0
    a, b = jnp.where(even, a, pltpu.roll(b, 32, 1)), jnp.where(even, pltpu.roll(a, 96, 1), b)
    c, d = jnp.where(even, c, pltpu.roll(d, 32, 1)), jnp.where(even, pltpu.roll(c, 96, 1), d)
    return a, b, c, d


def kernel(
    state_ref, noise_ref, pair_ref, contacts_ref, gain_ref, wqkv_ref, wout_ref, wb_ref, out_ref,
    x_ref, pair_buf, stage, bias_send, bias_all, qkv_send, qkv_recv, k_first, k_second, v_first, v_second,
    kcat, vcat, scores, probs, num, den, attn_send, attn_recv,
    pair_sem, bsend_sem, brecv_sem, fsend_sem, frecv_sem,
    ssend_sem, srecv_sem,
    ring_send, ring_recv, asend_sem, arecv_sem,
):
    z, c, s = lax.axis_index("row"), lax.axis_index("col"), lax.axis_index("smp")
    y, x0 = c // 4, c % 4
    kv_all = ((k_first, v_first), (k_second, v_second))

    def col_at(o, sign):
        return ((y + sign * o[0] + 4) % 4) * 4 + (x0 + sign * o[1] + 4) % 4

    def drain(ref, sem):
        pltpu.make_async_copy(ref, ref, sem).wait()

    barrier = pltpu.get_barrier_semaphore()
    for o in OFFSETS:
        pl.semaphore_signal(barrier, inc=1, device_id={"col": col_at(o, 1)}, device_id_type=MESH)
    right, left = (z + 1) % NZ, (z + NZ - 1) % NZ
    pl.semaphore_signal(barrier, inc=1, device_id={"row": right}, device_id_type=MESH)
    pl.semaphore_signal(barrier, inc=1, device_id={"row": left}, device_id_type=MESH)
    pl.semaphore_signal(barrier, inc=1, device_id={"smp": 1 - s}, device_id_type=MESH)

    def pair_copy(ch):
        return pltpu.make_async_copy(
            pair_ref.at[pl.ds(s * BLK + ch * CH, CH)], pair_buf.at[pl.ds(ch * CH, CH)], pair_sem.at[ch]
        )

    for ch in range(CHUNKS):
        pair_copy(ch).start()

    lane = lax.broadcasted_iota(jnp.int32, (ROWS, 128), 1)

    def project(step):
        x = x_ref[...]
        mean = jnp.mean(x, axis=-1, keepdims=True)
        var = jnp.mean((x - mean) ** 2, axis=-1, keepdims=True)
        h = ((x - mean) * lax.rsqrt(var + 1e-05) * gain_ref[...]).astype(BF)
        for part in (1, 2, 0):
            y3 = jnp.dot(h, wqkv_ref[:, part * DS : (part + 1) * DS], preferred_element_type=F32)
            if part == 0:
                y3 = y3 * 0.25
            for t in range(4):
                tiles = [y3[k * ROWS : (k + 1) * ROWS, t * 128 : (t + 1) * 128] for k in range(SAMP)]
                for u, tile in enumerate(swap4(tiles, lane)):
                    qkv_send[step, 4 * t + u, part] = tile.astype(BF)

    def rows_of(col):
        return pl.ds(pl.multiple_of(col * ROWS, ROWS), ROWS)

    def spread(step):
        dst, sem = qkv_recv.at[step, :, c // 8, rows_of(c % 8), :], srecv_sem.at[step]
        for o in OFFSETS:
            to = col_at(o, 1)
            pltpu.make_async_remote_copy(
                src_ref=qkv_send.at[step, to],
                dst_ref=dst,
                send_sem=ssend_sem.at[step],
                recv_sem=sem,
                device_id={"col": to},
                device_id_type=MESH,
            ).start()
        pltpu.make_async_copy(qkv_send.at[step, c], dst, sem).start()

    def ring_copy(step, kv, way, t, j, plane):
        dst = kv_all[step][kv].at[pl.ds(2 * plane + j * (2 // J), 2 // J)]
        src = qkv_recv.at[step, kv + 1, pl.ds(j * (2 // J), 2 // J)] if t == 0 else dst
        return pltpu.make_async_remote_copy(
            src_ref=src,
            dst_ref=dst,
            send_sem=ring_send.at[step, kv, way, t, j],
            recv_sem=ring_recv.at[step, kv, way, t, j],
            device_id={"row": right if way == 0 else left},
            device_id_type=MESH,
        )

    def ring_plane(way, t):
        return (z - t + NZ) % NZ if way == 0 else (z + t) % NZ

    def ring_used(kv, way, t, j):
        return t < 3 or (way == kv if J == 1 else (j < J // 2) == (way == 0))

    def ring_turn(step, kv, t):
        for j in range(J):
            for way in range(2):
                if not ring_used(kv, way, t, j):
                    continue
                if t > 0:
                    ring_copy(step, kv, way, t - 1, j, ring_plane(way, t)).wait_recv()
                ring_copy(step, kv, way, t, j, ring_plane(way, t)).start()

    def ring_finish(step, kv):
        for t in (2, 3):
            for way in range(2):
                for j in range(J):
                    if ring_used(kv, way, t, j) and not (t == 2 and ring_used(kv, way, 3, j)):
                        ring_copy(step, kv, way, t, j, ring_plane(way, t + 1)).wait_recv()

    def make_bias():
        wt = wb_ref[...]

        def chunk(ch, carry):
            pair_copy(ch).wait()
            for i in range(CH):
                stage[i * HEADS : (i + 1) * HEADS, :] = lax.dot_general(
                    wt, pair_buf[ch * CH + i], NT, preferred_element_type=F32
                )
            for h in range(HEADS):
                tile = stage[pl.ds(h, CH, stride=HEADS), :]
                bias_send[h // 2, h % 2, pl.ds(pl.multiple_of(ch * CH, CH), CH), :] = tile.astype(BF)
            return carry

        for g in range(PIECES):
            lax.fori_loop(g * CHUNKS // PIECES, (g + 1) * CHUNKS // PIECES, chunk, 0)
            part = pl.ds(g * BLK // PIECES, BLK // PIECES)
            for o in OFFSETS:
                to = col_at(o, 1)
                pltpu.make_async_remote_copy(
                    src_ref=bias_send.at[to, :, part, :],
                    dst_ref=bias_all.at[s, c, :, part, :],
                    send_sem=bsend_sem,
                    recv_sem=brecv_sem.at[c],
                    device_id={"col": to},
                    device_id_type=MESH,
                ).start()
        pltpu.make_async_copy(bias_send.at[c], bias_all.at[s, c], brecv_sem.at[c]).start()

    def pass_bias(col):
        drain(bias_all.at[s, col], brecv_sem.at[col])
        pltpu.make_async_remote_copy(
            src_ref=bias_all.at[s, col],
            dst_ref=bias_all.at[s, col],
            send_sem=fsend_sem,
            recv_sem=frecv_sem,
            device_id={"smp": 1 - s},
            device_id_type=MESH,
        ).start()

    def slot_of(qb, slot):
        return contacts_ref[slot, 2 * z + qb]

    def place_bias():
        for qb in range(2):
            for slot in range(KMAX):
                kb = slot_of(qb, slot)
                at = jnp.maximum(kb, 0)
                for hh in range(2):
                    tile = jnp.where(kb >= 0, bias_all[qb, at, hh].astype(F32).T, F32(-1e30))
                    kcat[qb, hh, slot * BLK : (slot + 1) * BLK, 128:] = tile.astype(BF)

    def block_of(step, kv, kb):
        return kv_all[step][kv][jnp.maximum(kb, 0)]

    def place_keys(step):
        for qb in range(2):
            for slot in range(KMAX):
                tile = block_of(step, 0, slot_of(qb, slot))
                for hh in range(2):
                    kcat[qb, hh, slot * BLK : (slot + 1) * BLK, :128] = tile

    def place_values(step):
        for qb in range(2):
            for slot in range(KMAX):
                tile = block_of(step, 1, slot_of(qb, slot))
                vcat[qb, slot * BLK : (slot + 1) * BLK, :128] = tile

    wide = lax.broadcasted_iota(jnp.int32, (BLK, 128), 1)
    diagonal = (lax.broadcasted_iota(jnp.int32, (BLK, 128), 0) == wide).astype(F32).astype(BF)

    def soften(step, lo, hi):
        def unit(it, carry):
            qb, hh = it // 2, it % 2
            q = qkv_recv[step, 0, qb]
            rows = []
            for k in range(SAMP):
                pick = (wide // HD == 2 * k + hh).astype(F32).astype(BF)
                rows.append(jnp.concatenate([q * pick, diagonal], axis=1))
            qs = jnp.concatenate(rows, axis=0)
            for n in range(KEYS // 256):
                cols = slice(n * 256, (n + 1) * 256)
                scores[:, cols] = lax.dot_general(qs, kcat[qb, hh, cols, :], NT, preferred_element_type=F32)
            for k in range(0, SAMP * BLK, STRIP):
                strip = scores[k : k + STRIP, :]
                top = jnp.max(strip, axis=-1, keepdims=True)
                probs[it, k : k + STRIP, :] = jnp.exp(strip - top).astype(BF)
            return carry

        lax.fori_loop(lo, hi, unit, 0)

    def mix(step):
        def unit(it, carry):
            qb, hh = it // 2, it % 2
            both = jnp.dot(probs[it], vcat[qb], preferred_element_type=F32)
            at = pl.ds(pl.multiple_of(qb * BLK, BLK), BLK)
            n, d = num[at, :], den[at, :]
            for k in range(SAMP):
                pick = wide // HD == 2 * k + hh
                part = both[k * BLK : (k + 1) * BLK]
                n = jnp.where(pick, part[:, :128], n)
                d = jnp.where(pick, part[:, 128:], d)
            num[at, :] = n
            den[at, :] = d
            return carry

        lax.fori_loop(0, 4, unit, 0)
        attn_send[step] = (num[...] / den[...]).astype(BF)

    def give_back(step):
        for o in OFFSETS:
            to = col_at(o, 1)
            pltpu.make_async_remote_copy(
                src_ref=attn_send.at[step, rows_of(to), :],
                dst_ref=attn_recv.at[step, c],
                send_sem=asend_sem.at[step],
                recv_sem=arecv_sem.at[step],
                device_id={"col": to},
                device_id_type=MESH,
            ).start()
        pltpu.make_async_copy(
            attn_send.at[step, rows_of(c), :], attn_recv.at[step, c], arecv_sem.at[step]
        ).start()
        drain(attn_recv.at[step], arecv_sem.at[step])

    def update(step):
        columns = []
        for t in range(4):
            tiles = [attn_recv[step, 4 * t + u].astype(F32) for u in range(4)]
            columns.append(swap4(tiles, lane))
        attn = jnp.concatenate(
            [jnp.concatenate([columns[t][k] for t in range(4)], axis=1) for k in range(SAMP)], axis=0
        ).astype(BF)
        out = jnp.dot(attn, wout_ref[...], preferred_element_type=F32)
        return x_ref[...] + out + 0.5 * 0.5**step * noise_ref[step]

    x_ref[...] = state_ref[...]
    vcat[:, :, 128:] = jnp.ones((2, KEYS, 128), BF)
    num[...] = jnp.zeros_like(num)
    den[...] = jnp.ones_like(den)
    project(0)
    pl.semaphore_wait(barrier, len(OFFSETS) + 3)
    for step in range(STEPS):
        if step:
            project(step)
        spread(step)
        if step == 0:
            make_bias()
        drain(qkv_recv.at[step], srecv_sem.at[step])
        ring_turn(step, 0, 0)
        ring_turn(step, 1, 0)
        for kv in range(2):
            kv_all[step][kv][pl.ds(2 * z, 2)] = qkv_recv[step, kv + 1]
        for t in range(1, 4):
            ring_turn(step, 0, t)
            ring_turn(step, 1, t)
        ring_finish(step, 0)
        place_keys(step)
        if step == 0:
            pass_bias(c)
            for o in reversed(OFFSETS):
                pass_bias(col_at(o, -1))
            drain(bias_all.at[1 - s], frecv_sem)
            place_bias()
        soften(step, 0, 4)
        ring_finish(step, 1)
        place_values(step)
        mix(step)
        give_back(step)
        x = update(step)
        if step < STEPS - 1:
            x_ref[...] = x
        else:
            out_ref[...] = x

    drain(bias_send.at[pl.ds(0, NC - 1)], bsend_sem)
    drain(bias_all.at[0], fsend_sem)
    for step in range(STEPS):
        drain(qkv_send.at[step, pl.ds(0, NC - 1)], ssend_sem.at[step])
        drain(attn_send.at[step, pl.ds(0, (NC - 1) * ROWS), :], asend_sem.at[step])
        for kv in range(2):
            for way in range(2):
                for t in range(4):
                    for j in range(J):
                        if ring_used(kv, way, t, j):
                            ring_copy(step, kv, way, t, j, ring_plane(way, t)).wait_send()


def body(state, noise, pair, contacts, norm_gain, w_qkv, w_out, w_bias):
    vmem = pl.BlockSpec(memory_space=pltpu.VMEM)
    dma = pltpu.SemaphoreType.DMA
    out = pl.pallas_call(
        kernel,
        out_shape=jax.ShapeDtypeStruct((SAMP * ROWS, DS), F32),
        in_specs=[
            vmem, vmem, pl.BlockSpec(memory_space=pltpu.HBM), pl.BlockSpec(memory_space=pltpu.SMEM),
            vmem, vmem, vmem, vmem,
        ],
        out_specs=vmem,
        scratch_shapes=[
            pltpu.VMEM((SAMP * ROWS, DS), F32),
            pltpu.VMEM((BLK, BLK, CP), BF),
            pltpu.VMEM((CH * HEADS, BLK), F32),
            pltpu.VMEM((NC, 2, BLK, BLK), BF),
            pltpu.VMEM((2, NC, 2, BLK, BLK), BF),
            pltpu.VMEM((STEPS, NC, 3, ROWS, 128), BF),
            pltpu.VMEM((STEPS, 3, 2, BLK, 128), BF),
            pltpu.VMEM((NC, BLK, 128), BF),
            pltpu.VMEM((NC, BLK, 128), BF),
            pltpu.VMEM((NC, BLK, 128), BF),
            pltpu.VMEM((NC, BLK, 128), BF),
            pltpu.VMEM((2, 2, KEYS, 256), BF),
            pltpu.VMEM((2, KEYS, 256), BF),
            pltpu.VMEM((SAMP * BLK, KEYS), F32),
            pltpu.VMEM((4, SAMP * BLK, KEYS), BF),
            pltpu.VMEM((2 * BLK, 128), F32),
            pltpu.VMEM((2 * BLK, 128), F32),
            pltpu.VMEM((STEPS, 2 * BLK, 128), BF),
            pltpu.VMEM((STEPS, NC, ROWS, 128), BF),
            dma((CHUNKS,)),
            dma,
            dma((NC,)),
            dma,
            dma,
            dma((STEPS,)),
            dma((STEPS,)),
            dma((STEPS, 2, 2, 4, J)),
            dma((STEPS, 2, 2, 4, J)),
            dma((STEPS,)),
            dma((STEPS,)),
        ],
        compiler_params=pltpu.CompilerParams(
            collective_id=0, has_side_effects=True, vmem_limit_bytes=56 * 1024 * 1024
        ),
        name="denoise",
    )(
        state.reshape(SAMP * ROWS, DS),
        noise.reshape(STEPS, SAMP * ROWS, DS),
        pair,
        contacts.T,
        norm_gain.reshape(1, DS),
        w_qkv,
        w_out,
        w_bias.T,
    )
    return out.reshape(SAMP, ROWS, DS)


def solution(mesh):
    in_specs = (
        P("smp", ("row", "col"), None),
        P(None, "smp", ("row", "col"), None),
        P("row", "col", None),
        P(),
        P(),
        P(),
        P(),
        P(),
    )
    out_specs = P("smp", ("row", "col"), None)
    return jax.shard_map(body, mesh=mesh, in_specs=in_specs, out_specs=out_specs, check_vma=False)
```

```python
import jax
import jax.numpy as jnp
from jax import lax
from jax.experimental import pallas as pl
from jax.experimental.pallas import tpu as pltpu
from jax.sharding import PartitionSpec as P


STEPS = 2
NZ, NC = 8, 16
SAMP, ROWS, DS = 4, 16, 512
HEADS, HD, CP = 32, 16, 128
BLK, KMAX = 128, 6
KEYS = KMAX * BLK
CHUNKS = 8
CH = BLK // CHUNKS
PIECES = 1
EARLY = 3
FIRST = tuple((0, w, j) for j in range(2) for w in (1, -1))
LATER = tuple((kv, o * w, w, j) for o in (1, 2) for kv in range(2) for j in range(2) for w in (1, -1)) + tuple(
    (kv, 3 * w, w, j) for kv in range(2) for w, j in ((1, 0), (-1, 1))
)
COMES = (1, -1, 2, -2, 3, -3, 4)
STRIP = 64
MESH = pl.DeviceIdType.MESH
BF, F32 = jnp.bfloat16, jnp.float32
NT = (((1,), (1,)), ((), ()))

OFFSETS = sorted(
    ((dy, dx) for dy in range(4) for dx in range(4) if (dy, dx) != (0, 0)),
    key=lambda o: -(min(o[0], 4 - o[0]) + min(o[1], 4 - o[1])),
)


def swap4(tiles, lane):
    a, b, c, d = tiles
    low = lane < 64
    a, c = jnp.where(low, a, pltpu.roll(c, 64, 1)), jnp.where(low, pltpu.roll(a, 64, 1), c)
    b, d = jnp.where(low, b, pltpu.roll(d, 64, 1)), jnp.where(low, pltpu.roll(b, 64, 1), d)
    even = (lane // 32) % 2 == 0
    a, b = jnp.where(even, a, pltpu.roll(b, 32, 1)), jnp.where(even, pltpu.roll(a, 96, 1), b)
    c, d = jnp.where(even, c, pltpu.roll(d, 32, 1)), jnp.where(even, pltpu.roll(c, 96, 1), d)
    return a, b, c, d


def kernel(
    state_hbm, noise_hbm, pair_ref, contacts_ref, gain_ref, wqkv_hbm, wout_hbm, wb_ref, out_ref,
    noise_ref, wqkv_ref, wout_ref, load_sem,
    x_ref, pair_buf, stage, bias_send, bias_all, qkv_send, qkv_recv, k_first, k_second, v_first, v_second,
    kcat, vcat, scores, probs, num, den, attn_send, attn_recv,
    pair_sem, bsend_sem, brecv_sem, fsend_sem, frecv_sem,
    ssend_sem, srecv_sem, krecv_sem,
    ring_send, ring_recv, asend_sem, arecv_sem,
):
    z, c, s = lax.axis_index("row"), lax.axis_index("col"), lax.axis_index("smp")
    y, x0 = c // 4, c % 4
    kv_all = ((k_first, v_first), (k_second, v_second))

    def col_at(o, sign):
        return ((y + sign * o[0] + 4) % 4) * 4 + (x0 + sign * o[1] + 4) % 4

    def drain(ref, sem):
        pltpu.make_async_copy(ref, ref, sem).wait()

    waited = set()
    barrier = pltpu.get_barrier_semaphore()
    for o in OFFSETS:
        pl.semaphore_signal(barrier, inc=1, device_id={"col": col_at(o, 1)}, device_id_type=MESH)
    for d in range(1, NZ):
        pl.semaphore_signal(barrier, inc=1, device_id={"row": (z + d) % NZ}, device_id_type=MESH)
    pl.semaphore_signal(barrier, inc=1, device_id={"smp": 1 - s}, device_id_type=MESH)

    def pair_copy(ch):
        return pltpu.make_async_copy(
            pair_ref.at[pl.ds(s * BLK + ch * CH, CH)], pair_buf.at[pl.ds(ch * CH, CH)], pair_sem.at[ch]
        )


    loads = [
        pltpu.make_async_copy(src, dst, load_sem.at[k])
        for k, (src, dst) in enumerate(
            ((state_hbm, x_ref), (wqkv_hbm, wqkv_ref), (wout_hbm, wout_ref), (noise_hbm, noise_ref))
        )
    ]

    for load in loads[:2]:
        load.start()
    for ch in range(CHUNKS):
        pair_copy(ch).start()
    for load in loads[2:]:
        load.start()

    lane = lax.broadcasted_iota(jnp.int32, (ROWS, 128), 1)

    def project(step):
        x = x_ref[...]
        mean = jnp.mean(x, axis=-1, keepdims=True)
        var = jnp.mean((x - mean) ** 2, axis=-1, keepdims=True)
        h = ((x - mean) * lax.rsqrt(var + 1e-05) * gain_ref[...]).astype(BF)
        for part in (1, 2, 0):
            y3 = jnp.dot(h, wqkv_ref[:, part * DS : (part + 1) * DS], preferred_element_type=F32)
            if part == 0:
                y3 = y3 * 0.25
            for t in range(4):
                tiles = [y3[k * ROWS : (k + 1) * ROWS, t * 128 : (t + 1) * 128] for k in range(SAMP)]
                for u, tile in enumerate(swap4(tiles, lane)):
                    qkv_send[step, 4 * t + u, (part + 2) % 3] = tile.astype(BF)
            if part == 1:
                if step == 0:
                    lax.fori_loop(0, EARLY, chunk, 0)
                    pl.semaphore_wait(barrier, len(OFFSETS) + NZ)
                spread(step, 0, 1, krecv_sem.at[step])
        spread(step, 1, 2, srecv_sem.at[step])

    def rows_of(col):
        return pl.ds(pl.multiple_of(col * ROWS, ROWS), ROWS)

    def spread(step, lo, n, sem):
        dst = qkv_recv.at[step, pl.ds(lo, n), c // 8, rows_of(c % 8), :]
        for o in OFFSETS:
            to = col_at(o, 1)
            pltpu.make_async_remote_copy(
                src_ref=qkv_send.at[step, to, pl.ds(lo, n)],
                dst_ref=dst,
                send_sem=ssend_sem.at[step],
                recv_sem=sem,
                device_id={"col": to},
                device_id_type=MESH,
            ).start()
        pltpu.make_async_copy(qkv_send.at[step, c, pl.ds(lo, n)], dst, sem).start()

    def z_copy(step, kv, origin, hop, j):
        dst = kv_all[step][kv].at[2 * ((z - origin + NZ) % NZ) + j]
        index = (origin + hop) % NZ
        return pltpu.make_async_remote_copy(
            src_ref=dst if origin else qkv_recv.at[step, kv, j],
            dst_ref=dst,
            send_sem=ring_send.at[step, kv, index, j],
            recv_sem=ring_recv.at[step, kv, index, j],
            device_id={"row": (z + hop + NZ) % NZ},
            device_id_type=MESH,
        )

    def z_wait(step, kv, come, j):
        if (step, kv, come, j) not in waited:
            waited.add((step, kv, come, j))
            drain(kv_all[step][kv].at[2 * ((z - come + NZ) % NZ) + j], ring_recv.at[step, kv, come % NZ, j])

    wt = wb_ref[...]

    def chunk(ch, carry):
        pair_copy(ch).wait()
        for i in range(CH):
            stage[i * HEADS : (i + 1) * HEADS, :] = lax.dot_general(
                wt, pair_buf[ch * CH + i], NT, preferred_element_type=F32
            )
        for h in range(HEADS):
            tile = stage[pl.ds(h, CH, stride=HEADS), :]
            bias_send[h // 2, h % 2, pl.ds(pl.multiple_of(ch * CH, CH), CH), :] = tile.astype(BF)
        return carry

    def make_bias():

        def turn(to):
            for hh in range(2):
                bias_send[to, hh] = bias_send[to, hh].astype(F32).T.astype(BF)

        for g in range(PIECES):
            lax.fori_loop(EARLY, CHUNKS, chunk, 0)
            part = pl.ds(g * BLK // PIECES, BLK // PIECES)
            for o in OFFSETS:
                to = col_at(o, 1)
                turn(to)
                pltpu.make_async_remote_copy(
                    src_ref=bias_send.at[to, :, part, :],
                    dst_ref=bias_all.at[s, c, :, part, :],
                    send_sem=bsend_sem,
                    recv_sem=brecv_sem.at[c],
                    device_id={"col": to},
                    device_id_type=MESH,
                ).start()
        turn(c)
        pltpu.make_async_copy(bias_send.at[c], bias_all.at[s, c], brecv_sem.at[c]).start()

    def pass_bias(col):
        drain(bias_all.at[s, col], brecv_sem.at[col])
        pltpu.make_async_remote_copy(
            src_ref=bias_all.at[s, col],
            dst_ref=bias_all.at[s, col],
            send_sem=fsend_sem,
            recv_sem=frecv_sem,
            device_id={"smp": 1 - s},
            device_id_type=MESH,
        ).start()

    def slot_of(qb, slot):
        return contacts_ref[slot, 2 * z + qb]

    def place_bias():
        for qb in range(2):
            for slot in range(KMAX):
                kb = slot_of(qb, slot)
                at = jnp.maximum(kb, 0)
                for hh in range(2):
                    tile = jnp.where(kb >= 0, bias_all[qb, at, hh].astype(F32), F32(-1e30))
                    kcat[qb, hh, slot * BLK : (slot + 1) * BLK, 128:] = tile.astype(BF)

    def block_of(step, kv, kb):
        return kv_all[step][kv][jnp.maximum(kb, 0)]

    def place_keys(step):
        for qb in range(2):
            for slot in range(KMAX):
                tile = block_of(step, 0, slot_of(qb, slot))
                for hh in range(2):
                    kcat[qb, hh, slot * BLK : (slot + 1) * BLK, :128] = tile

    def place_values(step):
        for qb in range(2):
            for slot in range(KMAX):
                tile = block_of(step, 1, slot_of(qb, slot))
                vcat[qb, slot * BLK : (slot + 1) * BLK, :128] = tile

    wide = lax.broadcasted_iota(jnp.int32, (BLK, 128), 1)
    diagonal = (lax.broadcasted_iota(jnp.int32, (BLK, 128), 0) == wide).astype(F32).astype(BF)

    def soften(step, lo, hi):
        def unit(it, carry):
            qb, hh = it // 2, it % 2
            q = qkv_recv[step, 2, qb]
            rows = []
            for k in range(SAMP):
                pick = (wide // HD == 2 * k + hh).astype(F32).astype(BF)
                rows.append(jnp.concatenate([q * pick, diagonal], axis=1))
            qs = jnp.concatenate(rows, axis=0)
            for n in range(KEYS // 256):
                cols = slice(n * 256, (n + 1) * 256)
                scores[:, cols] = lax.dot_general(qs, kcat[qb, hh, cols, :], NT, preferred_element_type=F32)
            for k in range(0, SAMP * BLK, STRIP):
                strip = scores[k : k + STRIP, :]
                top = jnp.max(strip, axis=-1, keepdims=True)
                probs[it, k : k + STRIP, :] = jnp.exp(strip - top).astype(BF)
            return carry

        lax.fori_loop(lo, hi, unit, 0)

    def mix(step):
        def unit(it, carry):
            qb, hh = it // 2, it % 2
            both = jnp.dot(probs[it], vcat[qb], preferred_element_type=F32)
            at = pl.ds(pl.multiple_of(qb * BLK, BLK), BLK)
            n, d = num[at, :], den[at, :]
            for k in range(SAMP):
                pick = wide // HD == 2 * k + hh
                part = both[k * BLK : (k + 1) * BLK]
                n = jnp.where(pick, part[:, :128], n)
                d = jnp.where(pick, part[:, 128:], d)
            num[at, :] = n
            den[at, :] = d
            return carry

        lax.fori_loop(0, 4, unit, 0)
        attn_send[step] = (num[...] / den[...]).astype(BF)

    def give_back(step):
        for o in OFFSETS:
            to = col_at(o, 1)
            pltpu.make_async_remote_copy(
                src_ref=attn_send.at[step, rows_of(to), :],
                dst_ref=attn_recv.at[step, c],
                send_sem=asend_sem.at[step],
                recv_sem=arecv_sem.at[step],
                device_id={"col": to},
                device_id_type=MESH,
            ).start()
        pltpu.make_async_copy(
            attn_send.at[step, rows_of(c), :], attn_recv.at[step, c], arecv_sem.at[step]
        ).start()
        drain(attn_recv.at[step], arecv_sem.at[step])

    def update(step):
        columns = []
        for t in range(4):
            tiles = [attn_recv[step, 4 * t + u].astype(F32) for u in range(4)]
            columns.append(swap4(tiles, lane))
        attn = jnp.concatenate(
            [jnp.concatenate([columns[t][k] for t in range(4)], axis=1) for k in range(SAMP)], axis=0
        ).astype(BF)
        out = jnp.dot(attn, wout_ref[...], preferred_element_type=F32)
        return x_ref[...] + out + 0.5 * 0.5**step * noise_ref[step]

    for k in range(2):
        loads[k].wait()
    vcat[:, :, 128:] = jnp.ones((2, KEYS, 128), BF)
    num[...] = jnp.zeros_like(num)
    den[...] = jnp.ones_like(den)
    for step in range(STEPS):
        project(step)
        if step == 0:
            make_bias()
        for kv in range(2):
            if kv == 0:
                drain(qkv_recv.at[step, 0], krecv_sem.at[step])
            else:
                drain(qkv_recv.at[step, pl.ds(1, 2)], srecv_sem.at[step])
            for origin, hop, j in FIRST:
                z_copy(step, kv, origin, hop, j).start()
            kv_all[step][kv][pl.ds(2 * z, 2)] = qkv_recv[step, kv]
        for kv, origin, hop, j in LATER:
            z_wait(step, kv, origin, j)
            z_copy(step, kv, origin, hop, j).start()
        for come in COMES:
            for j in range(2):
                z_wait(step, 0, come, j)
        place_keys(step)
        if step == 0:
            pass_bias(c)
            for o in reversed(OFFSETS):
                pass_bias(col_at(o, -1))
            drain(bias_all.at[1 - s], frecv_sem)
            place_bias()
        soften(step, 0, 4)
        for come in COMES:
            for j in range(2):
                z_wait(step, 1, come, j)
        place_values(step)
        mix(step)
        give_back(step)
        if step == 0:
            for k in (2, 3):
                loads[k].wait()
        x = update(step)
        if step < STEPS - 1:
            x_ref[...] = x
        else:
            out_ref[...] = x

    drain(bias_send.at[pl.ds(0, NC - 1)], bsend_sem)
    drain(bias_all.at[0], fsend_sem)
    for step in range(STEPS):
        drain(qkv_send.at[step, pl.ds(0, NC - 1)], ssend_sem.at[step])
        drain(attn_send.at[step, pl.ds(0, (NC - 1) * ROWS), :], asend_sem.at[step])
        for kv, origin, hop, j in tuple((kv, *f) for kv in range(2) for f in FIRST) + LATER:
            z_copy(step, kv, origin, hop, j).wait_send()


def body(state, noise, pair, contacts, norm_gain, w_qkv, w_out, w_bias):
    vmem = pl.BlockSpec(memory_space=pltpu.VMEM)
    hbm = pl.BlockSpec(memory_space=pltpu.HBM)
    dma = pltpu.SemaphoreType.DMA
    out = pl.pallas_call(
        kernel,
        out_shape=jax.ShapeDtypeStruct((SAMP * ROWS, DS), F32),
        in_specs=[
            hbm, hbm, hbm, pl.BlockSpec(memory_space=pltpu.SMEM), vmem, hbm, hbm, vmem,
        ],
        out_specs=vmem,
        scratch_shapes=[
            pltpu.VMEM((STEPS, SAMP * ROWS, DS), F32),
            pltpu.VMEM((DS, 3 * DS), BF),
            pltpu.VMEM((DS, DS), BF),
            dma((4,)),
            pltpu.VMEM((SAMP * ROWS, DS), F32),
            pltpu.VMEM((BLK, BLK, CP), BF),
            pltpu.VMEM((CH * HEADS, BLK), F32),
            pltpu.VMEM((NC, 2, BLK, BLK), BF),
            pltpu.VMEM((2, NC, 2, BLK, BLK), BF),
            pltpu.VMEM((STEPS, NC, 3, ROWS, 128), BF),
            pltpu.VMEM((STEPS, 3, 2, BLK, 128), BF),
            pltpu.VMEM((NC, BLK, 128), BF),
            pltpu.VMEM((NC, BLK, 128), BF),
            pltpu.VMEM((NC, BLK, 128), BF),
            pltpu.VMEM((NC, BLK, 128), BF),
            pltpu.VMEM((2, 2, KEYS, 256), BF),
            pltpu.VMEM((2, KEYS, 256), BF),
            pltpu.VMEM((SAMP * BLK, KEYS), F32),
            pltpu.VMEM((4, SAMP * BLK, KEYS), BF),
            pltpu.VMEM((2 * BLK, 128), F32),
            pltpu.VMEM((2 * BLK, 128), F32),
            pltpu.VMEM((STEPS, 2 * BLK, 128), BF),
            pltpu.VMEM((STEPS, NC, ROWS, 128), BF),
            dma((CHUNKS,)),
            dma,
            dma((NC,)),
            dma,
            dma,
            dma((STEPS,)),
            dma((STEPS,)),
            dma((STEPS,)),
            dma((STEPS, 2, NZ, 2)),
            dma((STEPS, 2, NZ, 2)),
            dma((STEPS,)),
            dma((STEPS,)),
        ],
        compiler_params=pltpu.CompilerParams(
            collective_id=0, has_side_effects=True, vmem_limit_bytes=56 * 1024 * 1024
        ),
        name="denoise",
    )(
        state.reshape(SAMP * ROWS, DS),
        noise.reshape(STEPS, SAMP * ROWS, DS),
        pair,
        contacts.T,
        norm_gain.reshape(1, DS),
        w_qkv,
        w_out,
        w_bias.T,
    )
    return out.reshape(SAMP, ROWS, DS)


def solution(mesh):
    in_specs = (
        P("smp", ("row", "col"), None),
        P(None, "smp", ("row", "col"), None),
        P("row", "col", None),
        P(),
        P(),
        P(),
        P(),
        P(),
    )
    out_specs = P("smp", ("row", "col"), None)
    return jax.shard_map(body, mesh=mesh, in_specs=in_specs, out_specs=out_specs, check_vma=False)
```

```python
import jax
import jax.numpy as jnp
from jax import lax
from jax.experimental import pallas as pl
from jax.experimental.pallas import tpu as pltpu
from jax.sharding import PartitionSpec as P


STEPS = 2
NZ, NC = 8, 16
SAMP, ROWS, DS = 4, 16, 512
HEADS, HD, CP = 32, 16, 128
BLK, KMAX = 128, 6
KEYS = KMAX * BLK
CHUNKS = 8
CH = BLK // CHUNKS
PIECES = 1
EARLY = 3
FIRST = tuple((0, w, j) for j in range(2) for w in (1, -1))
LATER = tuple((kv, o * w, w, j) for o in (1, 2) for kv in range(2) for j in range(2) for w in (1, -1)) + tuple(
    (kv, 3 * w, w, j) for kv in range(2) for w, j in ((1, 0), (-1, 1))
)
COMES = (1, -1, 2, -2, 3, -3, 4)
STRIP = 64
MESH = pl.DeviceIdType.MESH
BF, F32 = jnp.bfloat16, jnp.float32
NT = (((1,), (1,)), ((), ()))

OFFSETS = sorted(
    ((dy, dx) for dy in range(4) for dx in range(4) if (dy, dx) != (0, 0)),
    key=lambda o: -(min(o[0], 4 - o[0]) + min(o[1], 4 - o[1])),
)


def swap4(tiles, lane):
    a, b, c, d = tiles
    low = lane < 64
    a, c = jnp.where(low, a, pltpu.roll(c, 64, 1)), jnp.where(low, pltpu.roll(a, 64, 1), c)
    b, d = jnp.where(low, b, pltpu.roll(d, 64, 1)), jnp.where(low, pltpu.roll(b, 64, 1), d)
    even = (lane // 32) % 2 == 0
    a, b = jnp.where(even, a, pltpu.roll(b, 32, 1)), jnp.where(even, pltpu.roll(a, 96, 1), b)
    c, d = jnp.where(even, c, pltpu.roll(d, 32, 1)), jnp.where(even, pltpu.roll(c, 96, 1), d)
    return a, b, c, d


def kernel(
    state_hbm, noise_hbm, pair_ref, contacts_ref, gain_ref, wqkv_hbm, wout_hbm, wb_ref, out_ref,
    noise_ref, wqkv_ref, wout_ref, load_sem,
    x_ref, pair_buf, stage, bias_send, bias_all, qkv_send, qkv_recv, k_first, k_second, v_first, v_second,
    kcat, vcat, scores, probs, num, den, attn_send, attn_recv,
    pair_sem, bsend_sem, brecv_sem, fsend_sem, frecv_sem,
    ssend_sem, srecv_sem, krecv_sem,
    ring_send, ring_recv, asend_sem, arecv_sem,
):
    z, c, s = lax.axis_index("row"), lax.axis_index("col"), lax.axis_index("smp")
    y, x0 = c // 4, c % 4
    kv_all = ((k_first, v_first), (k_second, v_second))

    def col_at(o, sign):
        return ((y + sign * o[0] + 4) % 4) * 4 + (x0 + sign * o[1] + 4) % 4

    def drain(ref, sem):
        pltpu.make_async_copy(ref, ref, sem).wait()

    waited = set()
    barrier = pltpu.get_barrier_semaphore()
    for o in OFFSETS:
        pl.semaphore_signal(barrier, inc=1, device_id={"col": col_at(o, 1)}, device_id_type=MESH)
    for d in range(1, NZ):
        pl.semaphore_signal(barrier, inc=1, device_id={"row": (z + d) % NZ}, device_id_type=MESH)
    pl.semaphore_signal(barrier, inc=1, device_id={"smp": 1 - s}, device_id_type=MESH)

    def pair_copy(ch):
        return pltpu.make_async_copy(
            pair_ref.at[pl.ds(s * BLK + ch * CH, CH)], pair_buf.at[pl.ds(ch * CH, CH)], pair_sem.at[ch]
        )


    loads = [
        pltpu.make_async_copy(src, dst, load_sem.at[k])
        for k, (src, dst) in enumerate(
            ((state_hbm, x_ref), (wqkv_hbm, wqkv_ref), (wout_hbm, wout_ref), (noise_hbm, noise_ref))
        )
    ]

    for load in loads[:2]:
        load.start()
    for ch in range(CHUNKS):
        pair_copy(ch).start()
    for load in loads[2:]:
        load.start()

    lane = lax.broadcasted_iota(jnp.int32, (ROWS, 128), 1)

    def project(step):
        x = x_ref[...]
        mean = jnp.mean(x, axis=-1, keepdims=True)
        var = jnp.mean((x - mean) ** 2, axis=-1, keepdims=True)
        h = ((x - mean) * lax.rsqrt(var + 1e-05) * gain_ref[...]).astype(BF)
        for part in (1, 2, 0):
            y3 = jnp.dot(h, wqkv_ref[:, part * DS : (part + 1) * DS], preferred_element_type=F32)
            if part == 0:
                y3 = y3 * 0.25
            for t in range(4):
                tiles = [y3[k * ROWS : (k + 1) * ROWS, t * 128 : (t + 1) * 128] for k in range(SAMP)]
                for u, tile in enumerate(swap4(tiles, lane)):
                    qkv_send[step, 4 * t + u, (part + 2) % 3] = tile.astype(BF)
            if part == 1:
                if step == 0:
                    lax.fori_loop(0, EARLY, chunk, 0)
                    pl.semaphore_wait(barrier, len(OFFSETS) + NZ)
                spread(step, 0, 1, krecv_sem.at[step])
        spread(step, 1, 2, srecv_sem.at[step])

    def rows_of(col):
        return pl.ds(pl.multiple_of(col * ROWS, ROWS), ROWS)

    def spread(step, lo, n, sem):
        dst = qkv_recv.at[step, pl.ds(lo, n), c // 8, rows_of(c % 8), :]
        for o in OFFSETS:
            to = col_at(o, 1)
            pltpu.make_async_remote_copy(
                src_ref=qkv_send.at[step, to, pl.ds(lo, n)],
                dst_ref=dst,
                send_sem=ssend_sem.at[step],
                recv_sem=sem,
                device_id={"col": to},
                device_id_type=MESH,
            ).start()
        pltpu.make_async_copy(qkv_send.at[step, c, pl.ds(lo, n)], dst, sem).start()

    def z_copy(step, kv, origin, hop, j):
        dst = kv_all[step][kv].at[2 * ((z - origin + NZ) % NZ) + j]
        index = (origin + hop) % NZ
        return pltpu.make_async_remote_copy(
            src_ref=dst if origin else qkv_recv.at[step, kv, j],
            dst_ref=dst,
            send_sem=ring_send.at[step, kv, index, j],
            recv_sem=ring_recv.at[step, kv, index, j],
            device_id={"row": (z + hop + NZ) % NZ},
            device_id_type=MESH,
        )

    def z_wait(step, kv, come, j):
        if (step, kv, come, j) not in waited:
            waited.add((step, kv, come, j))
            drain(kv_all[step][kv].at[2 * ((z - come + NZ) % NZ) + j], ring_recv.at[step, kv, come % NZ, j])

    wt = wb_ref[...]

    def chunk(ch, carry):
        pair_copy(ch).wait()
        for i in range(CH):
            stage[i * HEADS : (i + 1) * HEADS, :] = lax.dot_general(
                wt, pair_buf[ch * CH + i], NT, preferred_element_type=F32
            )
        for h in range(HEADS):
            tile = stage[pl.ds(h, CH, stride=HEADS), :]
            bias_send[h // 2, h % 2, pl.ds(pl.multiple_of(ch * CH, CH), CH), :] = tile.astype(BF)
        return carry

    def make_bias():

        def turn(to):
            for hh in range(2):
                bias_send[to, hh] = bias_send[to, hh].astype(F32).T.astype(BF)

        for g in range(PIECES):
            lax.fori_loop(EARLY, CHUNKS, chunk, 0)
            part = pl.ds(g * BLK // PIECES, BLK // PIECES)
            for o in OFFSETS:
                to = col_at(o, 1)
                turn(to)
                pltpu.make_async_remote_copy(
                    src_ref=bias_send.at[to, :, part, :],
                    dst_ref=bias_all.at[s, c, :, part, :],
                    send_sem=bsend_sem,
                    recv_sem=brecv_sem.at[c],
                    device_id={"col": to},
                    device_id_type=MESH,
                ).start()
        turn(c)
        pltpu.make_async_copy(bias_send.at[c], bias_all.at[s, c], brecv_sem.at[c]).start()

    def pass_bias(col):
        drain(bias_all.at[s, col], brecv_sem.at[col])
        pltpu.make_async_remote_copy(
            src_ref=bias_all.at[s, col],
            dst_ref=bias_all.at[s, col],
            send_sem=fsend_sem,
            recv_sem=frecv_sem,
            device_id={"smp": 1 - s},
            device_id_type=MESH,
        ).start()

    def slot_of(qb, slot):
        return contacts_ref[slot, 2 * z + qb]

    def place_bias():
        for qb in range(2):
            for slot in range(KMAX):
                kb = slot_of(qb, slot)
                at = jnp.maximum(kb, 0)
                for hh in range(2):
                    tile = jnp.where(kb >= 0, bias_all[qb, at, hh].astype(F32), F32(-1e30))
                    kcat[qb, hh, slot * BLK : (slot + 1) * BLK, 128:] = tile.astype(BF)

    def block_of(step, kv, kb):
        return kv_all[step][kv][jnp.maximum(kb, 0)]

    def place_keys(step):
        for qb in range(2):
            for slot in range(KMAX):
                tile = block_of(step, 0, slot_of(qb, slot))
                for hh in range(2):
                    kcat[qb, hh, slot * BLK : (slot + 1) * BLK, :128] = tile

    def place_values(step):
        for qb in range(2):
            for slot in range(KMAX):
                tile = block_of(step, 1, slot_of(qb, slot))
                vcat[qb, slot * BLK : (slot + 1) * BLK, :128] = tile

    wide = lax.broadcasted_iota(jnp.int32, (BLK, 128), 1)
    diagonal = (lax.broadcasted_iota(jnp.int32, (BLK, 128), 0) == wide).astype(F32).astype(BF)

    def soften(step, lo, hi):
        def unit(it, carry):
            qb, hh = it // 2, it % 2
            q = qkv_recv[step, 2, qb]
            rows = []
            for k in range(SAMP):
                pick = (wide // HD == 2 * k + hh).astype(F32).astype(BF)
                rows.append(jnp.concatenate([q * pick, diagonal], axis=1))
            qs = jnp.concatenate(rows, axis=0)
            for n in range(KEYS // 256):
                cols = slice(n * 256, (n + 1) * 256)
                scores[:, cols] = lax.dot_general(qs, kcat[qb, hh, cols, :], NT, preferred_element_type=F32)
            for k in range(0, SAMP * BLK, STRIP):
                strip = scores[k : k + STRIP, :]
                top = jnp.max(strip, axis=-1, keepdims=True)
                probs[it, k : k + STRIP, :] = jnp.exp(strip - top).astype(BF)
            return carry

        lax.fori_loop(lo, hi, unit, 0)

    def mix(step):
        def unit(it, carry):
            qb, hh = it // 2, it % 2
            both = jnp.dot(probs[it], vcat[qb], preferred_element_type=F32)
            at = pl.ds(pl.multiple_of(qb * BLK, BLK), BLK)
            n, d = num[at, :], den[at, :]
            for k in range(SAMP):
                pick = wide // HD == 2 * k + hh
                part = both[k * BLK : (k + 1) * BLK]
                n = jnp.where(pick, part[:, :128], n)
                d = jnp.where(pick, part[:, 128:], d)
            num[at, :] = n
            den[at, :] = d
            return carry

        lax.fori_loop(0, 4, unit, 0)
        attn_send[step] = (num[...] / den[...]).astype(BF)

    def give_back(step):
        for o in OFFSETS:
            to = col_at(o, 1)
            pltpu.make_async_remote_copy(
                src_ref=attn_send.at[step, rows_of(to), :],
                dst_ref=attn_recv.at[step, c],
                send_sem=asend_sem.at[step],
                recv_sem=arecv_sem.at[step],
                device_id={"col": to},
                device_id_type=MESH,
            ).start()
        pltpu.make_async_copy(
            attn_send.at[step, rows_of(c), :], attn_recv.at[step, c], arecv_sem.at[step]
        ).start()
        drain(attn_recv.at[step], arecv_sem.at[step])

    def update(step):
        columns = []
        for t in range(4):
            tiles = [attn_recv[step, 4 * t + u].astype(F32) for u in range(4)]
            columns.append(swap4(tiles, lane))
        attn = jnp.concatenate(
            [jnp.concatenate([columns[t][k] for t in range(4)], axis=1) for k in range(SAMP)], axis=0
        ).astype(BF)
        out = jnp.dot(attn, wout_ref[...], preferred_element_type=F32)
        out = x_ref[...] + out
        return out + 0.5 * 0.5**step * noise_ref[step] if step < STEPS - 1 else out

    for k in range(2):
        loads[k].wait()
    vcat[:, :, 128:] = jnp.ones((2, KEYS, 128), BF)
    num[...] = jnp.zeros_like(num)
    den[...] = jnp.ones_like(den)
    for step in range(STEPS):
        project(step)
        if step == 0:
            make_bias()
        for kv in range(2):
            if kv == 0:
                drain(qkv_recv.at[step, 0], krecv_sem.at[step])
            else:
                drain(qkv_recv.at[step, pl.ds(1, 2)], srecv_sem.at[step])
            for origin, hop, j in FIRST:
                z_copy(step, kv, origin, hop, j).start()
            kv_all[step][kv][pl.ds(2 * z, 2)] = qkv_recv[step, kv]
        for kv, origin, hop, j in LATER:
            z_wait(step, kv, origin, j)
            z_copy(step, kv, origin, hop, j).start()
        for come in COMES:
            for j in range(2):
                z_wait(step, 0, come, j)
        place_keys(step)
        if step == 0:
            pass_bias(c)
            for o in reversed(OFFSETS):
                pass_bias(col_at(o, -1))
            drain(bias_all.at[1 - s], frecv_sem)
            place_bias()
        soften(step, 0, 4)
        for come in COMES:
            for j in range(2):
                z_wait(step, 1, come, j)
        place_values(step)
        mix(step)
        give_back(step)
        if step == 0:
            for k in (2, 3):
                loads[k].wait()
        x = update(step)
        if step < STEPS - 1:
            x_ref[...] = x
        else:
            out_ref[...] = x

    drain(bias_send.at[pl.ds(0, NC - 1)], bsend_sem)
    drain(bias_all.at[0], fsend_sem)
    for step in range(STEPS):
        drain(qkv_send.at[step, pl.ds(0, NC - 1)], ssend_sem.at[step])
        drain(attn_send.at[step, pl.ds(0, (NC - 1) * ROWS), :], asend_sem.at[step])
        for kv, origin, hop, j in tuple((kv, *f) for kv in range(2) for f in FIRST) + LATER:
            z_copy(step, kv, origin, hop, j).wait_send()


def body(state, noise, pair, contacts, norm_gain, w_qkv, w_out, w_bias):
    vmem = pl.BlockSpec(memory_space=pltpu.VMEM)
    hbm = pl.BlockSpec(memory_space=pltpu.HBM)
    dma = pltpu.SemaphoreType.DMA
    out = pl.pallas_call(
        kernel,
        out_shape=jax.ShapeDtypeStruct((SAMP * ROWS, DS), F32),
        in_specs=[
            hbm, hbm, hbm, pl.BlockSpec(memory_space=pltpu.SMEM), vmem, hbm, hbm, vmem,
        ],
        out_specs=vmem,
        scratch_shapes=[
            pltpu.VMEM((STEPS, SAMP * ROWS, DS), F32),
            pltpu.VMEM((DS, 3 * DS), BF),
            pltpu.VMEM((DS, DS), BF),
            dma((4,)),
            pltpu.VMEM((SAMP * ROWS, DS), F32),
            pltpu.VMEM((BLK, BLK, CP), BF),
            pltpu.VMEM((CH * HEADS, BLK), F32),
            pltpu.VMEM((NC, 2, BLK, BLK), BF),
            pltpu.VMEM((2, NC, 2, BLK, BLK), BF),
            pltpu.VMEM((STEPS, NC, 3, ROWS, 128), BF),
            pltpu.VMEM((STEPS, 3, 2, BLK, 128), BF),
            pltpu.VMEM((NC, BLK, 128), BF),
            pltpu.VMEM((NC, BLK, 128), BF),
            pltpu.VMEM((NC, BLK, 128), BF),
            pltpu.VMEM((NC, BLK, 128), BF),
            pltpu.VMEM((2, 2, KEYS, 256), BF),
            pltpu.VMEM((2, KEYS, 256), BF),
            pltpu.VMEM((SAMP * BLK, KEYS), F32),
            pltpu.VMEM((4, SAMP * BLK, KEYS), BF),
            pltpu.VMEM((2 * BLK, 128), F32),
            pltpu.VMEM((2 * BLK, 128), F32),
            pltpu.VMEM((STEPS, 2 * BLK, 128), BF),
            pltpu.VMEM((STEPS, NC, ROWS, 128), BF),
            dma((CHUNKS,)),
            dma,
            dma((NC,)),
            dma,
            dma,
            dma((STEPS,)),
            dma((STEPS,)),
            dma((STEPS,)),
            dma((STEPS, 2, NZ, 2)),
            dma((STEPS, 2, NZ, 2)),
            dma((STEPS,)),
            dma((STEPS,)),
        ],
        compiler_params=pltpu.CompilerParams(
            collective_id=0, has_side_effects=True, vmem_limit_bytes=56 * 1024 * 1024
        ),
        name="denoise",
    )(
        state.reshape(SAMP * ROWS, DS),
        noise.reshape(STEPS, SAMP * ROWS, DS),
        pair,
        contacts.T,
        norm_gain.reshape(1, DS),
        w_qkv,
        w_out,
        w_bias.T,
    )
    return out.reshape(SAMP, ROWS, DS) + 0.5 * 0.5 ** (STEPS - 1) * noise[STEPS - 1]


def solution(mesh):
    in_specs = (
        P("smp", ("row", "col"), None),
        P(None, "smp", ("row", "col"), None),
        P("row", "col", None),
        P(),
        P(),
        P(),
        P(),
        P(),
    )
    out_specs = P("smp", ("row", "col"), None)
    return jax.shard_map(body, mesh=mesh, in_specs=in_specs, out_specs=out_specs, check_vma=False)
```
